32 devices in a mesh: ctx: 16 (over z, y, x), head: 2 (over core).
Axes of the slice: x: 2, y: 2, z: 4, core: 2. Of those that a mesh axis runs over, the one named last changes fastest.
Arguments:
- queries: bfloat16 [2048, 8192], P('ctx', 'head'), may hold values from -15 to 15
- keys: bfloat16 [2048, 1024], P('ctx', 'head'), may hold values from -6 to 6
- values: bfloat16 [2048, 1024], P('ctx', 'head'), may hold values from -6 to 6
- window: int32 [8], P('head'), may hold values from 512 to 1024, as said below
Outputs:
- loss: float32 [], replicated
- grad_queries: float32 [2048, 8192], P('ctx', 'head')
- grad_keys: float32 [2048, 1024], P('ctx', 'head')
- grad_values: float32 [2048, 1024], P('ctx', 'head')
The draws below stay inside these ranges and needn't reach their ends.
Inputs may be any that keep to these rules, and one draw needn't show every extreme that they name: Some key-value head's window is exactly 1024.
All inputs are finite; a program needn't handle non-finite values.
Results may differ from the reference program's by a relative error of at most 0.0095.
Values may be sent and summed in bfloat16 or wider, within the bound.
A program may use at most 64 MiB of HBM per device.

```python
import math
import jax
import jax.numpy as jnp
from jax import lax

QH = 64
KVH = 8
HD = 128
WINDOW = 1024
SEQ = 2048


def query_key_pair(key):
    base_key = jax.random.fold_in(key, 11)
    key_q, key_k = jax.random.split(base_key, 2)
    query_part = 2.5 * jnp.clip(jax.random.normal(key_q, (SEQ, QH * HD), jnp.float32), -6.0, 6.0)
    key_part = jnp.clip(jax.random.normal(key_k, (SEQ, KVH * HD), jnp.float32), -6.0, 6.0)
    return (query_part, key_part)


def draw_queries(key, part):
    return query_key_pair(key)[0].astype(jnp.bfloat16)


def draw_keys(key, part):
    return query_key_pair(key)[1].astype(jnp.bfloat16)


def draw_window(key, part):
    lengths = jax.random.randint(jax.random.fold_in(key, 5), (KVH,), WINDOW // 2, WINDOW + 1)
    chosen = jax.random.randint(jax.random.fold_in(key, 6), (), 0, KVH)
    return jnp.where(jnp.arange(KVH) == chosen, WINDOW, lengths).astype(jnp.int32)


def block_levels(key, shape, shards, smallest, largest):
    def one(axis_at, parts):
        steps = jax.random.uniform(jax.random.fold_in(jax.random.fold_in(key, 6), axis_at), (parts,), jnp.float32, smallest / len(shards), largest / len(shards))
        return jnp.repeat(jnp.exp(steps), shape[axis_at] // parts).reshape((-1,) + (1,) * (len(shape) - axis_at - 1))

    factor_of = one(*shards[0])
    for cut in shards[1:]:
        factor_of = factor_of * one(*cut)
    return factor_of


def normal_values(key, shape, scale, reach, pieces=(), kind=jnp.bfloat16):
    drawn = jax.random.normal(key, shape, jnp.float32) * scale
    if len(pieces) > 0:
        drawn = block_levels(key, shape, pieces, -0.22, 0.18) * drawn
    return jnp.clip(drawn, min=-reach, max=reach).astype(kind)


def setup_inputs(seed: int = 0) -> dict:
    streams_of = jax.random.split(jax.random.key(seed), 5)
    queries = draw_queries(jax.random.fold_in(streams_of[4], 71), 0)
    keys = draw_keys(jax.random.fold_in(streams_of[4], 71), 0)
    values = normal_values(streams_of[2], (SEQ, KVH * HD), 1.0, 6.0, ((0, 16), (1, 2)))
    window = draw_window(jax.random.fold_in(streams_of[4], 71), 0)
    return {"queries": queries, "keys": keys, "values": values, "window": window}


masked_score = -1e+30

def rounded(values_in):
    return lax.optimization_barrier(values_in.astype(jnp.bfloat16)).astype(jnp.float32)

def one_group(operands):
    group_q, group_k, group_v, group_w = operands
    block_rows = math.gcd(512, SEQ)
    inverse_root = 1.0 / math.sqrt(HD)
    query_f = group_q.astype(jnp.float32)
    keys_f = group_k.astype(jnp.float32)
    values_f = group_v.astype(jnp.float32)
    positions = jnp.arange(SEQ, dtype=jnp.int32)
    grad_keys = jnp.zeros((SEQ, HD), jnp.float32)
    grad_values = jnp.zeros((SEQ, HD), jnp.float32)
    grad_rows = []
    square_sum = jnp.zeros((), jnp.float32)
    for block_index in range(SEQ // block_rows):
        low_row = block_index * block_rows
        high_row = low_row + block_rows
        start_key = max(0, low_row - WINDOW)
        query_block = query_f[low_row:high_row]
        query_pos = positions[low_row:high_row]
        key_pos = positions[:high_row]
        visible = key_pos[None, :] <= query_pos[:, None]
        scores = jnp.einsum('tgd,sd->gts', query_block, keys_f[:high_row]) * inverse_root
        scores = jnp.where(visible[None], scores, masked_score)
        exponent = jnp.where(visible[None], jnp.exp(scores - lax.optimization_barrier(jnp.max(scores, axis=-1, keepdims=True))), 0.0)
        teacher_sum = jnp.einsum('gts,sd->tgd', rounded(exponent), values_f[:high_row])
        teacher_out = rounded(teacher_sum / lax.optimization_barrier(jnp.sum(exponent, axis=-1)).T[..., None])
        near_pos = positions[start_key:high_row]
        allowed = (near_pos[None, :] <= query_pos[:, None]) & (near_pos[None, :] > query_pos[:, None] - group_w)
        near_keys = keys_f[start_key:high_row]
        near_values = values_f[start_key:high_row]
        scores = jnp.einsum('tgd,sd->gts', query_block, near_keys) * inverse_root
        scores = jnp.where(allowed[None], scores, masked_score)
        exponent = jnp.where(allowed[None], jnp.exp(scores - lax.optimization_barrier(jnp.max(scores, axis=-1, keepdims=True))), 0.0)
        totals = lax.optimization_barrier(jnp.sum(exponent, axis=-1))
        student_out = jnp.einsum('gts,sd->tgd', rounded(exponent), near_values) / totals.T[..., None]
        difference = student_out - teacher_out
        square_sum = square_sum + jnp.sum(difference * difference)
        grad_out = rounded(difference)
        probabilities = exponent / totals[..., None]
        grad_values = grad_values.at[start_key:high_row].add(jnp.einsum('gts,tgd->sd', rounded(probabilities), grad_out))
        row_dot = lax.optimization_barrier(jnp.sum(difference * student_out, axis=-1))
        grad_probs = jnp.einsum('tgd,sd->gts', grad_out, near_values)
        grad_scores = rounded(probabilities * (grad_probs - row_dot.T[..., None]))
        grad_rows.append(jnp.einsum('gts,sd->tgd', grad_scores, near_keys) * inverse_root)
        grad_keys = grad_keys.at[start_key:high_row].add(jnp.einsum('gts,tgd->sd', grad_scores, query_block) * inverse_root)
    return (jnp.concatenate(grad_rows, axis=0), grad_keys, grad_values, square_sum)

def reference(queries, keys, values, window):
    group_size = QH // KVH
    grouped_q = queries.reshape(SEQ, KVH, group_size, HD).transpose(1, 0, 2, 3)
    grouped_k = keys.reshape(SEQ, KVH, HD).transpose(1, 0, 2)
    grouped_v = values.reshape(SEQ, KVH, HD).transpose(1, 0, 2)
    grad_q, grad_k, grad_v, squares = lax.map(one_group, (grouped_q, grouped_k, grouped_v, window))
    loss = jnp.sum(squares) / (SEQ * QH * HD)
    return (loss, grad_q.transpose(1, 0, 2, 3).reshape(SEQ, QH * HD), grad_k.transpose(1, 0, 2).reshape(SEQ, KVH * HD), grad_v.transpose(1, 0, 2).reshape(SEQ, KVH * HD))
```

```python
import functools
import math

import jax
import jax.numpy as jnp
from jax import lax
from jax.experimental import pallas as pl
from jax.experimental.pallas import tpu as pltpu
from jax.sharding import PartitionSpec as P

QH = 64
KVH = 8
HD = 128
WIN_MAX = 1024
WIN_MIN = 512
GS = QH // KVH

MESH = pl.DeviceIdType.MESH
NEG = -1e30
FLOOR = -1e20
F32 = jnp.float32
BF16 = jnp.bfloat16


def dot_nt(a, b):
    return lax.dot_general(a, b, (((1,), (1,)), ((), ())), preferred_element_type=F32)


def dot_nn(a, b):
    return jnp.dot(a, b, preferred_element_type=F32)


def kernel(
    G, NB, SH, T, D,
    w_ref, q_ref, k_ref, v_ref,
    dq_out, dkv_out, loss_out,
    qs, kvs, kts, vts, o_near, o_far, stats, dos, dqs, dkv_acc, dkv_send, dkv_recv, dkv_fin, loss_acc,
    q_send, q_recv, k_send, k_recv, v_send, v_recv, kv_send, kv_recv,
    g_send, g_recv, dq_send, dq_recv, f_send, f_recv, loc,
):
    R = G * SH
    NT = R // T
    QW = GS * HD
    me = lax.axis_index("ctx")
    z = me // G
    p = lax.rem(me, G)
    c = math.log2(math.e) / math.sqrt(HD)
    inv_root = 1.0 / math.sqrt(HD)

    def dev(zz, pp):
        return {"ctx": zz * G + pp}

    barrier = pltpu.get_barrier_semaphore()
    for o in range(1, G):
        pl.semaphore_signal(barrier, inc=1, device_id=dev(z, lax.rem(p + o, G)), device_id_type=MESH)

    def greet(o, carry):
        pl.semaphore_signal(barrier, inc=1, device_id=dev(lax.rem(z + o, NB), p), device_id_type=MESH)
        return carry

    lax.fori_loop(1, NB, greet, 0)
    pl.semaphore_wait(barrier, G - 1 + NB - 1)

    def my_rows(pp):
        return pl.ds(pl.multiple_of(pp * SH, SH), SH)

    def wide(pp):
        return pl.ds(pl.multiple_of(pp * QW, QW), QW)

    def narrow(pp):
        return pl.ds(pl.multiple_of(pp * HD, HD), HD)

    def kv_copy(src, part, o, send, recv):
        to = lax.rem(p + o, G)
        return pltpu.make_async_remote_copy(
            src_ref=src.at[:, narrow(to)],
            dst_ref=kvs.at[z, part, my_rows(p), :],
            send_sem=send.at[to], recv_sem=recv.at[p],
            device_id=dev(z, to), device_id_type=MESH)

    def q_copy(o):
        to = lax.rem(p + o, G)
        return pltpu.make_async_remote_copy(
            src_ref=q_ref.at[:, wide(to)],
            dst_ref=qs.at[my_rows(p), :],
            send_sem=q_send.at[to], recv_sem=q_recv.at[p],
            device_id=dev(z, to), device_id_type=MESH)

    def recv_kv(frm, part, recv):
        return pltpu.make_async_remote_copy(
            src_ref=kvs.at[z, part, my_rows(frm), :], dst_ref=kvs.at[z, part, my_rows(frm), :],
            send_sem=k_send.at[frm], recv_sem=recv.at[frm],
            device_id=dev(z, frm), device_id_type=MESH)

    for o in range(1, G):
        kv_copy(k_ref, 0, o, k_send, k_recv).start()
        kv_copy(v_ref, 1, o, v_send, v_recv).start()
    for o in range(1, G):
        q_copy(o).start()
    local = [
        pltpu.make_async_copy(k_ref.at[:, narrow(p)], kvs.at[z, 0, my_rows(p), :], loc.at[0]),
        pltpu.make_async_copy(v_ref.at[:, narrow(p)], kvs.at[z, 1, my_rows(p), :], loc.at[1]),
        pltpu.make_async_copy(q_ref.at[:, wide(p)], qs.at[my_rows(p), :], loc.at[2]),
    ]
    for one in local:
        one.start()

    stats[...] = jnp.zeros_like(stats)
    loss_acc[...] = jnp.zeros_like(loss_acc)

    def clear(h, carry):
        o_far[h] = jnp.zeros(o_far.shape[1:], F32)
        stats[h, pl.ds(2, 1), :] = jnp.full((1, R), FLOOR, F32)
        return carry

    lax.fori_loop(0, GS, clear, 0)

    for one in local:
        one.wait()
    for o in range(1, G):
        frm = lax.rem(p + o, G)
        recv_kv(frm, 0, k_recv).wait_recv()
        recv_kv(frm, 1, v_recv).wait_recv()

    def block_copy(src_block, to_z):
        return pltpu.make_async_remote_copy(
            src_ref=kvs.at[src_block], dst_ref=kvs.at[src_block],
            send_sem=kv_send.at[to_z], recv_sem=kv_recv.at[src_block],
            device_id=dev(to_z, p), device_id_type=MESH)

    def send_up(to_z, carry):
        block_copy(z, to_z).start()
        return carry

    lax.fori_loop(z + 1, NB, send_up, 0)
    for o in range(1, G):
        frm = lax.rem(p + o, G)
        pltpu.make_async_remote_copy(
            src_ref=qs.at[my_rows(frm), :], dst_ref=qs.at[my_rows(frm), :],
            send_sem=q_send.at[frm], recv_sem=q_recv.at[frm],
            device_id=dev(z, frm), device_id_type=MESH).wait_recv()

    window = w_ref[p]
    ramp = lax.broadcasted_iota(jnp.int32, (T, T), 1) - lax.broadcasted_iota(jnp.int32, (T, T), 0)

    def tiles_of(d, rt):
        found = []
        for kt in range(NT):
            delta = d * R + (rt - kt) * T
            if delta < 0:
                continue
            near = delta - (T - 1) < WIN_MAX
            far = delta + (T - 1) >= WIN_MIN
            found.append((kt, delta, near, far))
        return found

    def turn(ref_out, block, part):
        ref_out[...] = kvs[block, part].astype(F32).T.astype(BF16)

    def forward(h, d, rt, block, far_only=False):
        rows = slice(rt * T, (rt + 1) * T)
        q = qs[rows, narrow(h)]
        work = []
        for kt, delta, near, far in ([(kt, None, False, True) for kt in range(NT)] if far_only else tiles_of(d, rt)):
            keys = kvs[block, 0, kt * T:(kt + 1) * T, :]
            work.append((kt, delta, near, far, dot_nt(keys, q) * c))
        has_near = any(t[2] for t in work)
        has_far = any(t[3] for t in work)
        if has_near:
            m_s = None if d == 0 else stats[h, 0:1, rows]
            new_s = m_s
        if has_far:
            m_f = stats[h, 2:3, rows]
            new_f = m_f
        masks = []
        for kt, delta, near, far, s in work:
            mask = None
            if near and far:
                mask = ramp < window - delta
                s_near = jnp.where(mask, s, NEG)
                s_far = jnp.where(mask, NEG, s)
            elif near and delta == 0:
                s_near = jnp.where(ramp >= 0, s, NEG)
                mask = s_near
            else:
                s_near = s_far = s
            masks.append(mask)
            if near:
                top = jnp.max(s_near, axis=0, keepdims=True)
                new_s = top if new_s is None else jnp.maximum(new_s, top)
            if far:
                new_f = jnp.maximum(new_f, jnp.max(s_far, axis=0, keepdims=True))
        near_sum, far_sum, near_o, far_o = 0.0, 0.0, 0.0, 0.0
        for (kt, delta, near, far, s), mask in zip(work, masks):
            vt = vts[:, kt * T:(kt + 1) * T]
            if near and far:
                e = jnp.exp2(s - jnp.where(mask, new_s, new_f))
                p_near = jnp.where(mask, e, 0.0)
                p_far = jnp.where(mask, 0.0, e)
            elif near:
                p_near = jnp.exp2((mask if delta == 0 else s) - new_s)
            else:
                p_far = jnp.exp2(s - new_f)
            if near:
                near_sum = near_sum + jnp.sum(p_near, axis=0, keepdims=True)
                near_o = near_o + dot_nn(vt, p_near.astype(BF16))
            if far:
                far_sum = far_sum + jnp.sum(p_far, axis=0, keepdims=True)
                far_o = far_o + dot_nn(vt, p_far.astype(BF16))
        if has_near:
            if d == 0:
                stats[h, 1:2, rows] = near_sum
                o_near[h, :, rows] = near_o
            else:
                factor = jnp.exp2(m_s - new_s)
                stats[h, 1:2, rows] = stats[h, 1:2, rows] * factor + near_sum
                o_near[h, :, rows] = o_near[h, :, rows] * factor + near_o
            stats[h, 0:1, rows] = new_s
        if has_far:
            factor = jnp.exp2(m_f - new_f)
            stats[h, 3:4, rows] = stats[h, 3:4, rows] * factor + far_sum
            o_far[h, :, rows] = o_far[h, :, rows] * factor + far_o
            stats[h, 2:3, rows] = new_f

    def heads(fn):
        def step(h, carry):
            fn(h)
            return carry
        lax.fori_loop(0, GS, step, 0)

    def arrive(block):
        block_copy(block, z).wait_recv()

    for d in range(0, min(D, NB - 1) + 1):
        @pl.when(z >= d)
        def _():
            block = z - d
            if d > 0:
                arrive(block)
            turn(vts, block, 1)
            for rt in range(NT):
                heads(lambda h: forward(h, d, rt, block))

    if NB - 1 > D:
        def far_block(d, carry):
            block = z - d
            arrive(block)
            turn(vts, block, 1)
            for rt in range(NT):
                heads(lambda h: forward(h, None, rt, block, True))
            return carry
        lax.fori_loop(D + 1, z + 1, far_block, 0)

    def middle(h, rt):
        rows = slice(rt * T, (rt + 1) * T)
        m_s, l_s = stats[h, 0:1, rows], stats[h, 1:2, rows]
        m_f, l_f = stats[h, 2:3, rows], stats[h, 3:4, rows]
        m_t = jnp.maximum(m_s, m_f)
        a_s, a_f = jnp.exp2(m_s - m_t), jnp.exp2(m_f - m_t)
        total = l_s * a_s + l_f * a_f
        near = o_near[h, :, rows]
        student = near / l_s
        teacher = (near * a_s + o_far[h, :, rows] * a_f) / total
        diff = student - teacher.astype(BF16).astype(F32)
        loss_acc[...] += jnp.sum((diff * diff).reshape(HD // 8, 8, T), axis=0)
        stats[h, 4:5, rows] = m_s + jnp.log2(l_s)
        stats[h, 5:6, rows] = jnp.sum(diff * student, axis=0, keepdims=True)
        dos[rows, narrow(h)] = diff.T.astype(BF16)
        o_near[h, :, rows] = jnp.zeros((HD, T), F32)

    for rt in range(NT):
        heads(lambda h: middle(h, rt))
    loss_out[...] = loss_acc[...]

    def backward(h, d, rt, block):
        rows = slice(rt * T, (rt + 1) * T)
        q = qs[rows, narrow(h)]
        do = dos[rows, narrow(h)]
        lse = stats[h, 4:5, rows]
        rd = stats[h, 5:6, rows]
        dq = o_near[h, :, rows]
        for kt, delta, near, far in tiles_of(d, rt):
            if not near:
                continue
            part = slice(kt * T, (kt + 1) * T)
            s = dot_nt(kvs[block, 0, part, :], q) * c
            if far:
                s = jnp.where(ramp < window - delta, s, NEG)
            elif delta == 0:
                s = jnp.where(ramp >= 0, s, NEG)
            w = jnp.exp2(s - lse)
            dp = dot_nt(kvs[block, 1, part, :], do)
            ds = (w * (dp - rd)).astype(BF16)
            dkv_acc[1, part, :] += dot_nn(w.astype(BF16), do)
            dkv_acc[0, part, :] += dot_nn(ds, q)
            dq = dq + dot_nn(kts[:, part], ds)
        if d == 0:
            dqs[rows, narrow(h)] = (dq * inv_root).T.astype(BF16)
        else:
            o_near[h, :, rows] = dq

    def term_copy(d, to_z):
        return pltpu.make_async_remote_copy(
            src_ref=dkv_send.at[d - 1], dst_ref=dkv_recv.at[d - 1],
            send_sem=g_send.at[d - 1], recv_sem=g_recv.at[d - 1],
            device_id=dev(to_z, p), device_id_type=MESH)

    def dq_copy(to):
        return pltpu.make_async_remote_copy(
            src_ref=dqs.at[my_rows(to), :], dst_ref=dq_out.at[p],
            send_sem=dq_send.at[to], recv_sem=dq_recv.at[p],
            device_id=dev(z, to), device_id_type=MESH)

    def dq_local(to):
        return pltpu.make_async_copy(dqs.at[my_rows(to), :], dq_out.at[p], loc.at[2])

    def fin_copy(to):
        return pltpu.make_async_remote_copy(
            src_ref=dkv_fin.at[:, my_rows(to), :], dst_ref=dkv_out.at[p],
            send_sem=f_send.at[to], recv_sem=f_recv.at[p],
            device_id=dev(z, to), device_id_type=MESH)

    def fin_local(to):
        return pltpu.make_async_copy(dkv_fin.at[:, my_rows(to), :], dkv_out.at[p], loc.at[3])

    for d in range(min(D, NB - 1), 0, -1):
        @pl.when(z >= d)
        def _():
            block = z - d
            dkv_acc[...] = jnp.zeros_like(dkv_acc)
            turn(kts, block, 0)
            for rt in range(NT):
                if any(t[2] for t in tiles_of(d, rt)):
                    heads(lambda h: backward(h, d, rt, block))
            dkv_send[d - 1, 0] = (dkv_acc[0] * inv_root).astype(BF16)
            dkv_send[d - 1, 1] = dkv_acc[1].astype(BF16)
            term_copy(d, z - d).start()

    dkv_acc[...] = jnp.zeros_like(dkv_acc)
    turn(kts, z, 0)
    for rt in range(NT):
        heads(lambda h: backward(h, 0, rt, z))
        for to in range(rt * T // SH, (rt + 1) * T // SH):
            @pl.when(p != to)
            def _():
                dq_copy(to).start()

            @pl.when(p == to)
            def _():
                dq_local(to).start()

    dkv_acc[0] = dkv_acc[0] * inv_root
    for d in range(1, min(D, NB - 1) + 1):
        @pl.when(z + d < NB)
        def _():
            term_copy(d, z).wait_recv()
            dkv_acc[...] += dkv_recv[d - 1].astype(F32)
    dkv_fin[...] = dkv_acc[...].astype(BF16)
    for to in range(G):
        @pl.when(p != to)
        def _():
            fin_copy(to).start()

        @pl.when(p == to)
        def _():
            fin_local(to).start()

    def drain_up(to_z, carry):
        block_copy(z, to_z).wait_send()
        return carry

    for o in range(1, G):
        kv_copy(k_ref, 0, o, k_send, k_recv).wait_send()
        kv_copy(v_ref, 1, o, v_send, v_recv).wait_send()
        q_copy(o).wait_send()
    lax.fori_loop(z + 1, NB, drain_up, 0)
    for d in range(1, min(D, NB - 1) + 1):
        @pl.when(z >= d)
        def _():
            term_copy(d, z - d).wait_send()
    dq_local(p).wait()
    fin_local(p).wait()
    for o in range(1, G):
        other = lax.rem(p + o, G)
        dq_copy(other).wait_send()
        fin_copy(other).wait_send()
        pltpu.make_async_remote_copy(
            src_ref=dq_out.at[other], dst_ref=dq_out.at[other],
            send_sem=dq_send.at[other], recv_sem=dq_recv.at[other],
            device_id=dev(z, other), device_id_type=MESH).wait_recv()
        pltpu.make_async_remote_copy(
            src_ref=dkv_out.at[other], dst_ref=dkv_out.at[other],
            send_sem=f_send.at[other], recv_sem=f_recv.at[other],
            device_id=dev(z, other), device_id_type=MESH).wait_recv()


def body(queries, keys, values, window):
    sh, key_width = keys.shape
    G = key_width // HD
    n_ctx = lax.axis_size("ctx")
    NB = n_ctx // G
    R = G * sh
    T = math.gcd(R, 256)
    D = (WIN_MAX - 1 + R - 1) // R
    DS = max(1, min(D, NB - 1))
    dma = pltpu.SemaphoreType.DMA
    any_spec = pl.BlockSpec(memory_space=pl.ANY)
    dq, dkv, loss_part = pl.pallas_call(
        functools.partial(kernel, G, NB, sh, T, D),
        out_shape=(
            jax.ShapeDtypeStruct((G, sh, GS * HD), BF16),
            jax.ShapeDtypeStruct((G, 2, sh, HD), BF16),
            jax.ShapeDtypeStruct((8, T), F32),
        ),
        in_specs=[pl.BlockSpec(memory_space=pltpu.SMEM), any_spec, any_spec, any_spec],
        out_specs=(any_spec, any_spec, pl.BlockSpec(memory_space=pltpu.VMEM)),
        scratch_shapes=[
            pltpu.VMEM((R, GS * HD), BF16),
            pltpu.VMEM((NB, 2, R, HD), BF16),
            pltpu.VMEM((HD, R), BF16),
            pltpu.VMEM((HD, R), BF16),
            pltpu.VMEM((GS, HD, R), F32),
            pltpu.VMEM((GS, HD, R), F32),
            pltpu.VMEM((GS, 8, R), F32),
            pltpu.VMEM((R, GS * HD), BF16),
            pltpu.VMEM((R, GS * HD), BF16),
            pltpu.VMEM((2, R, HD), F32),
            pltpu.VMEM((DS, 2, R, HD), BF16),
            pltpu.VMEM((DS, 2, R, HD), BF16),
            pltpu.VMEM((2, R, HD), BF16),
            pltpu.VMEM((8, T), F32),
            dma((G,)), dma((G,)), dma((G,)), dma((G,)), dma((G,)), dma((G,)),
            dma((NB,)), dma((NB,)),
            dma((DS,)), dma((DS,)),
            dma((G,)), dma((G,)), dma((G,)), dma((G,)),
            dma((4,)),
        ],
        compiler_params=pltpu.CompilerParams(
            collective_id=0, has_side_effects=True, vmem_limit_bytes=56 * 1024 * 1024),
    )(window, queries, keys, values)
    loss = lax.psum(jnp.sum(loss_part), ("ctx", "head")) / (sh * n_ctx * QH * HD)
    grad_q = dq.transpose(1, 0, 2).reshape(sh, -1).astype(F32)
    grads = dkv.transpose(1, 2, 0, 3).reshape(2, sh, -1).astype(F32)
    return (loss, grad_q, grads[0], grads[1])


def solution(mesh):
    return jax.shard_map(
        body,
        mesh=mesh,
        in_specs=(P("ctx", "head"), P("ctx", "head"), P("ctx", "head"), P("head")),
        out_specs=(P(), P("ctx", "head"), P("ctx", "head"), P("ctx", "head")),
        check_vma=False,
    )
```

```python
import functools
import math

import jax
import jax.numpy as jnp
from jax import lax
from jax.experimental import pallas as pl
from jax.experimental.pallas import tpu as pltpu
from jax.sharding import PartitionSpec as P

QH = 64
KVH = 8
HD = 128
WIN_MAX = 1024
WIN_MIN = 512
GS = QH // KVH

MESH = pl.DeviceIdType.MESH
NEG = -1e30
FLOOR = -1e20
F32 = jnp.float32
BF16 = jnp.bfloat16


def dot_nt(a, b):
    return lax.dot_general(a, b, (((1,), (1,)), ((), ())), preferred_element_type=F32)


def dot_nn(a, b):
    return jnp.dot(a, b, preferred_element_type=F32)


def kernel(
    G, NB, NH, SH, T, D,
    w_ref, q_ref, k_ref, v_ref,
    dq_out, dk_out, dv_out, loss_out,
    qs, kvs, kts, vts, o_near, o_far, stats, dos, dqs, dkv_acc, dkv_send, dkv_recv, dkv_fin, loss_acc, l_head, l_group, l_line,
    q_send, q_recv, k_send, k_recv, v_send, v_recv, kv_send, kv_recv,
    g_send, g_recv, dq_send, dq_recv, f_send, f_recv, e_send, e_recv, lh_send, lh_recv, lg_send, lg_recv, ll_send, ll_recv, loc,
):
    R = G * SH
    NT = R // T
    QW = GS * HD
    me = lax.axis_index("ctx")
    hd = lax.axis_index("head")
    z = me // G
    p = lax.rem(me, G)
    c = math.log2(math.e) / math.sqrt(HD)
    inv_root = 1.0 / math.sqrt(HD)

    def dev(zz, pp):
        return {"ctx": zz * G + pp}

    barrier = pltpu.get_barrier_semaphore()
    for o in range(1, G):
        pl.semaphore_signal(barrier, inc=1, device_id=dev(z, lax.rem(p + o, G)), device_id_type=MESH)

    def greet(o, carry):
        pl.semaphore_signal(barrier, inc=1, device_id=dev(lax.rem(z + o, NB), p), device_id_type=MESH)
        return carry

    lax.fori_loop(1, NB, greet, 0)
    for o in range(1, NH):
        pl.semaphore_signal(barrier, inc=1, device_id={"head": lax.rem(hd + o, NH)}, device_id_type=MESH)
    pl.semaphore_wait(barrier, G - 1 + NB - 1 + NH - 1)

    def my_rows(pp):
        return pl.ds(pl.multiple_of(pp * SH, SH), SH)

    def wide(pp):
        return pl.ds(pl.multiple_of(pp * QW, QW), QW)

    def narrow(pp):
        return pl.ds(pl.multiple_of(pp * HD, HD), HD)

    def kv_copy(src, part, o, send, recv):
        to = lax.rem(p + o, G)
        return pltpu.make_async_remote_copy(
            src_ref=src.at[:, narrow(to)],
            dst_ref=kvs.at[z, part, my_rows(p), :],
            send_sem=send.at[to], recv_sem=recv.at[p],
            device_id=dev(z, to), device_id_type=MESH)

    def q_copy(o):
        to = lax.rem(p + o, G)
        return pltpu.make_async_remote_copy(
            src_ref=q_ref.at[:, wide(to)],
            dst_ref=qs.at[my_rows(p), :],
            send_sem=q_send.at[to], recv_sem=q_recv.at[p],
            device_id=dev(z, to), device_id_type=MESH)

    def recv_kv(frm, part, recv):
        return pltpu.make_async_remote_copy(
            src_ref=kvs.at[z, part, my_rows(frm), :], dst_ref=kvs.at[z, part, my_rows(frm), :],
            send_sem=k_send.at[frm], recv_sem=recv.at[frm],
            device_id=dev(z, frm), device_id_type=MESH)

    for o in range(1, G):
        kv_copy(k_ref, 0, o, k_send, k_recv).start()
        kv_copy(v_ref, 1, o, v_send, v_recv).start()
    for o in range(1, G):
        q_copy(o).start()
    local = [
        pltpu.make_async_copy(k_ref.at[:, narrow(p)], kvs.at[z, 0, my_rows(p), :], loc.at[0]),
        pltpu.make_async_copy(v_ref.at[:, narrow(p)], kvs.at[z, 1, my_rows(p), :], loc.at[1]),
        pltpu.make_async_copy(q_ref.at[:, wide(p)], qs.at[my_rows(p), :], loc.at[2]),
    ]
    for one in local:
        one.start()

    stats[...] = jnp.zeros_like(stats)
    loss_acc[...] = jnp.zeros_like(loss_acc)

    def clear(h, carry):
        o_far[h] = jnp.zeros(o_far.shape[1:], F32)
        stats[h, pl.ds(2, 1), :] = jnp.full((1, R), FLOOR, F32)
        return carry

    lax.fori_loop(0, GS, clear, 0)

    for one in local:
        one.wait()
    for o in range(1, G):
        frm = lax.rem(p + o, G)
        recv_kv(frm, 0, k_recv).wait_recv()
        recv_kv(frm, 1, v_recv).wait_recv()

    def block_copy(src_block, to_z):
        return pltpu.make_async_remote_copy(
            src_ref=kvs.at[src_block], dst_ref=kvs.at[src_block],
            send_sem=kv_send.at[to_z], recv_sem=kv_recv.at[src_block],
            device_id=dev(to_z, p), device_id_type=MESH)

    def send_up(to_z, carry):
        block_copy(z, to_z).start()
        return carry

    lax.fori_loop(z + 1, NB, send_up, 0)
    for o in range(1, G):
        frm = lax.rem(p + o, G)
        pltpu.make_async_remote_copy(
            src_ref=qs.at[my_rows(frm), :], dst_ref=qs.at[my_rows(frm), :],
            send_sem=q_send.at[frm], recv_sem=q_recv.at[frm],
            device_id=dev(z, frm), device_id_type=MESH).wait_recv()

    window = w_ref[p]
    ramp = lax.broadcasted_iota(jnp.int32, (T, T), 1) - lax.broadcasted_iota(jnp.int32, (T, T), 0)

    def tiles_of(d, rt):
        found = []
        for kt in range(NT):
            delta = d * R + (rt - kt) * T
            if delta < 0:
                continue
            near = delta - (T - 1) < WIN_MAX
            far = delta + (T - 1) >= WIN_MIN
            found.append((kt, delta, near, far))
        return found

    def turn(ref_out, block, part):
        ref_out[...] = kvs[block, part].astype(F32).T.astype(BF16)

    def forward(h, d, rt, block, far_only=False):
        rows = slice(rt * T, (rt + 1) * T)
        q = qs[rows, narrow(h)]
        work = []
        for kt, delta, near, far in ([(kt, None, False, True) for kt in range(NT)] if far_only else tiles_of(d, rt)):
            keys = kvs[block, 0, kt * T:(kt + 1) * T, :]
            work.append((kt, delta, near, far, dot_nt(keys, q) * c))
        has_near = any(t[2] for t in work)
        has_far = any(t[3] for t in work)
        if has_near:
            m_s = None if d == 0 else stats[h, 0:1, rows]
            new_s = m_s
        if has_far:
            m_f = stats[h, 2:3, rows]
            new_f = m_f
        masks = []
        for kt, delta, near, far, s in work:
            mask = None
            if near and far:
                mask = ramp < window - delta
                s_near = jnp.where(mask, s, NEG)
                s_far = jnp.where(mask, NEG, s)
            elif near and delta == 0:
                s_near = jnp.where(ramp >= 0, s, NEG)
                mask = s_near
            else:
                s_near = s_far = s
            masks.append(mask)
            if near:
                top = jnp.max(s_near, axis=0, keepdims=True)
                new_s = top if new_s is None else jnp.maximum(new_s, top)
            if far:
                new_f = jnp.maximum(new_f, jnp.max(s_far, axis=0, keepdims=True))
        near_sum, far_sum, near_o, far_o = 0.0, 0.0, 0.0, 0.0
        for (kt, delta, near, far, s), mask in zip(work, masks):
            vt = vts[:, kt * T:(kt + 1) * T]
            if near and far:
                e = jnp.exp2(s - jnp.where(mask, new_s, new_f))
                p_near = jnp.where(mask, e, 0.0)
                p_far = jnp.where(mask, 0.0, e)
            elif near:
                p_near = jnp.exp2((mask if delta == 0 else s) - new_s)
            else:
                p_far = jnp.exp2(s - new_f)
            if near:
                near_sum = near_sum + jnp.sum(p_near, axis=0, keepdims=True)
                near_o = near_o + dot_nn(vt, p_near.astype(BF16))
            if far:
                far_sum = far_sum + jnp.sum(p_far, axis=0, keepdims=True)
                far_o = far_o + dot_nn(vt, p_far.astype(BF16))
        if has_near:
            if d == 0:
                stats[h, 1:2, rows] = near_sum
                o_near[h, :, rows] = near_o
            else:
                factor = jnp.exp2(m_s - new_s)
                stats[h, 1:2, rows] = stats[h, 1:2, rows] * factor + near_sum
                o_near[h, :, rows] = o_near[h, :, rows] * factor + near_o
            stats[h, 0:1, rows] = new_s
        if has_far:
            factor = jnp.exp2(m_f - new_f)
            stats[h, 3:4, rows] = stats[h, 3:4, rows] * factor + far_sum
            o_far[h, :, rows] = o_far[h, :, rows] * factor + far_o
            stats[h, 2:3, rows] = new_f

    def heads(fn):
        def step(h, carry):
            fn(h)
            return carry
        lax.fori_loop(0, GS, step, 0)

    def arrive(block):
        block_copy(block, z).wait_recv()

    for d in range(0, min(D, NB - 1) + 1):
        @pl.when(z >= d)
        def _():
            block = z - d
            if d > 0:
                arrive(block)
            turn(vts, block, 1)
            for rt in range(NT):
                heads(lambda h: forward(h, d, rt, block))

    if NB - 1 > D:
        def far_block(d, carry):
            block = z - d
            arrive(block)
            turn(vts, block, 1)
            for rt in range(NT):
                heads(lambda h: forward(h, None, rt, block, True))
            return carry
        lax.fori_loop(D + 1, z + 1, far_block, 0)

    def middle(h, rt):
        rows = slice(rt * T, (rt + 1) * T)
        m_s, l_s = stats[h, 0:1, rows], stats[h, 1:2, rows]
        m_f, l_f = stats[h, 2:3, rows], stats[h, 3:4, rows]
        m_t = jnp.maximum(m_s, m_f)
        a_s, a_f = jnp.exp2(m_s - m_t), jnp.exp2(m_f - m_t)
        total = l_s * a_s + l_f * a_f
        near = o_near[h, :, rows]
        student = near / l_s
        teacher = (near * a_s + o_far[h, :, rows] * a_f) / total
        diff = student - teacher.astype(BF16).astype(F32)
        loss_acc[...] += jnp.sum((diff * diff).reshape(HD // 8, 8, T), axis=0)
        stats[h, 4:5, rows] = m_s + jnp.log2(l_s)
        stats[h, 5:6, rows] = jnp.sum(diff * student, axis=0, keepdims=True)
        dos[rows, narrow(h)] = diff.T.astype(BF16)
        o_near[h, :, rows] = jnp.zeros((HD, T), F32)

    for rt in range(NT):
        heads(lambda h: middle(h, rt))
    head_loss = loss_acc[:, 0:128]
    for lane in range(128, T, 128):
        head_loss = head_loss + loss_acc[:, lane:lane + 128]
    l_head[hd] = head_loss

    def loss_copies(buf, count, mine, send, recv, where):
        def one(o, carry, act):
            to = lax.rem(mine + o, count)
            act(pltpu.make_async_remote_copy(
                src_ref=buf.at[mine], dst_ref=buf.at[mine],
                send_sem=send.at[to], recv_sem=recv.at[mine],
                device_id=where(to), device_id_type=MESH))
            return carry

        def got(o, carry):
            frm = lax.rem(mine + o, count)
            pltpu.make_async_remote_copy(
                src_ref=buf.at[frm], dst_ref=buf.at[frm],
                send_sem=send.at[frm], recv_sem=recv.at[frm],
                device_id=where(frm), device_id_type=MESH).wait_recv()
            return carry

        def start():
            lax.fori_loop(1, count, functools.partial(one, act=lambda x: x.start()), 0)

        def total():
            lax.fori_loop(1, count, got, 0)
            return lax.fori_loop(1, count, lambda i, t: t + buf[i], buf[0])

        def drain():
            lax.fori_loop(1, count, functools.partial(one, act=lambda x: x.wait_send()), 0)

        return start, total, drain

    loss_head = loss_copies(l_head, NH, hd, lh_send, lh_recv, lambda to: {"head": to})
    loss_group = loss_copies(l_group, G, p, lg_send, lg_recv, lambda to: dev(z, to))
    loss_line = loss_copies(l_line, NB, z, ll_send, ll_recv, lambda to: dev(to, p))
    loss_head[0]()

    def backward(h, d, rt, block):
        rows = slice(rt * T, (rt + 1) * T)
        q = qs[rows, narrow(h)]
        do = dos[rows, narrow(h)]
        lse = stats[h, 4:5, rows]
        rd = stats[h, 5:6, rows]
        dq = o_near[h, :, rows]
        for kt, delta, near, far in tiles_of(d, rt):
            if not near:
                continue
            part = slice(kt * T, (kt + 1) * T)
            s = dot_nt(kvs[block, 0, part, :], q) * c
            if far:
                s = jnp.where(ramp < window - delta, s, NEG)
            elif delta == 0:
                s = jnp.where(ramp >= 0, s, NEG)
            w = jnp.exp2(s - lse)
            dp = dot_nt(kvs[block, 1, part, :], do)
            ds = (w * (dp - rd)).astype(BF16)
            dkv_acc[1, part, :] += dot_nn(w.astype(BF16), do)
            dkv_acc[0, part, :] += dot_nn(ds, q)
            dq = dq + dot_nn(kts[:, part], ds)
        if d == 0:
            dqs[rows, narrow(h)] = (dq * inv_root).T.astype(BF16)
        else:
            o_near[h, :, rows] = dq

    def term_copy(d, to_z):
        return pltpu.make_async_remote_copy(
            src_ref=dkv_send.at[d - 1], dst_ref=dkv_recv.at[d - 1],
            send_sem=g_send.at[d - 1], recv_sem=g_recv.at[d - 1],
            device_id=dev(to_z, p), device_id_type=MESH)

    def dq_copy(to):
        return pltpu.make_async_remote_copy(
            src_ref=dqs.at[my_rows(to), :], dst_ref=dq_out.at[:, wide(p)],
            send_sem=dq_send.at[to], recv_sem=dq_recv.at[p],
            device_id=dev(z, to), device_id_type=MESH)

    def dq_local(to):
        return pltpu.make_async_copy(dqs.at[my_rows(to), :], dq_out.at[:, wide(p)], loc.at[2])

    def fin_copy(to, part):
        out, send, recv = ((dk_out, f_send, f_recv), (dv_out, e_send, e_recv))[part]
        return pltpu.make_async_remote_copy(
            src_ref=dkv_fin.at[part, my_rows(to), :], dst_ref=out.at[:, narrow(p)],
            send_sem=send.at[to], recv_sem=recv.at[p],
            device_id=dev(z, to), device_id_type=MESH)

    def fin_local(to, part):
        out = (dk_out, dv_out)[part]
        return pltpu.make_async_copy(
            dkv_fin.at[part, my_rows(to), :], out.at[:, narrow(p)], loc.at[part])

    for d in range(min(D, NB - 1), 0, -1):
        @pl.when(z >= d)
        def _():
            block = z - d
            dkv_acc[...] = jnp.zeros_like(dkv_acc)
            turn(kts, block, 0)
            for rt in range(NT):
                if any(t[2] for t in tiles_of(d, rt)):
                    heads(lambda h: backward(h, d, rt, block))
            dkv_send[d - 1, 0] = (dkv_acc[0] * inv_root).astype(BF16)
            dkv_send[d - 1, 1] = dkv_acc[1].astype(BF16)
            term_copy(d, z - d).start()

    l_group[p] = loss_head[1]()
    loss_group[0]()
    dkv_acc[...] = jnp.zeros_like(dkv_acc)
    turn(kts, z, 0)
    for rt in range(NT):
        heads(lambda h: backward(h, 0, rt, z))
        if rt == 0:
            l_line[z] = loss_group[1]()
            loss_line[0]()
        for to in range(rt * T // SH, (rt + 1) * T // SH):
            @pl.when(p != to)
            def _():
                dq_copy(to).start()

            @pl.when(p == to)
            def _():
                dq_local(to).start()

    dkv_acc[0] = dkv_acc[0] * inv_root
    for d in range(1, min(D, NB - 1) + 1):
        @pl.when(z + d < NB)
        def _():
            term_copy(d, z).wait_recv()
            dkv_acc[...] += dkv_recv[d - 1].astype(F32)
    dkv_fin[...] = dkv_acc[...].astype(BF16)
    for to in range(G):
        @pl.when(p != to)
        def _():
            fin_copy(to, 0).start()
            fin_copy(to, 1).start()

        @pl.when(p == to)
        def _():
            fin_local(to, 0).start()
            fin_local(to, 1).start()

    def drain_up(to_z, carry):
        block_copy(z, to_z).wait_send()
        return carry

    for o in range(1, G):
        kv_copy(k_ref, 0, o, k_send, k_recv).wait_send()
        kv_copy(v_ref, 1, o, v_send, v_recv).wait_send()
        q_copy(o).wait_send()
    lax.fori_loop(z + 1, NB, drain_up, 0)
    for d in range(1, min(D, NB - 1) + 1):
        @pl.when(z >= d)
        def _():
            term_copy(d, z - d).wait_send()
    dq_local(p).wait()
    fin_local(p, 0).wait()
    fin_local(p, 1).wait()
    loss_out[0, 0] = jnp.sum(loss_line[1]()) / (NB * R * QH * HD)
    for part in (loss_head, loss_group, loss_line):
        part[2]()
    for o in range(1, G):
        other = lax.rem(p + o, G)
        dq_copy(other).wait_send()
        for part in range(2):
            fin_copy(other, part).wait_send()
            out, send, recv = ((dk_out, f_send, f_recv), (dv_out, e_send, e_recv))[part]
            landed = out.at[:, narrow(other)]
            pltpu.make_async_remote_copy(
                src_ref=landed, dst_ref=landed, send_sem=send.at[other], recv_sem=recv.at[other],
                device_id=dev(z, other), device_id_type=MESH).wait_recv()
        landed = dq_out.at[:, wide(other)]
        pltpu.make_async_remote_copy(
            src_ref=landed, dst_ref=landed, send_sem=dq_send.at[other], recv_sem=dq_recv.at[other],
            device_id=dev(z, other), device_id_type=MESH).wait_recv()


def body(queries, keys, values, window):
    sh, key_width = keys.shape
    G = key_width // HD
    n_ctx = lax.axis_size("ctx")
    NB = n_ctx // G
    R = G * sh
    T = math.gcd(R, 256)
    D = (WIN_MAX - 1 + R - 1) // R
    DS = max(1, min(D, NB - 1))
    dma = pltpu.SemaphoreType.DMA
    any_spec = pl.BlockSpec(memory_space=pl.ANY)
    NH = lax.axis_size("head")
    dq, dk, dv, loss = pl.pallas_call(
        functools.partial(kernel, G, NB, NH, sh, T, D),
        out_shape=(
            jax.ShapeDtypeStruct((sh, G * GS * HD), BF16),
            jax.ShapeDtypeStruct((sh, G * HD), BF16),
            jax.ShapeDtypeStruct((sh, G * HD), BF16),
            jax.ShapeDtypeStruct((1, 1), F32),
        ),
        in_specs=[pl.BlockSpec(memory_space=pltpu.SMEM), any_spec, any_spec, any_spec],
        out_specs=(any_spec, any_spec, any_spec, pl.BlockSpec(memory_space=pltpu.SMEM)),
        scratch_shapes=[
            pltpu.VMEM((R, GS * HD), BF16),
            pltpu.VMEM((NB, 2, R, HD), BF16),
            pltpu.VMEM((HD, R), BF16),
            pltpu.VMEM((HD, R), BF16),
            pltpu.VMEM((GS, HD, R), F32),
            pltpu.VMEM((GS, HD, R), F32),
            pltpu.VMEM((GS, 8, R), F32),
            pltpu.VMEM((R, GS * HD), BF16),
            pltpu.VMEM((R, GS * HD), BF16),
            pltpu.VMEM((2, R, HD), F32),
            pltpu.VMEM((DS, 2, R, HD), BF16),
            pltpu.VMEM((DS, 2, R, HD), BF16),
            pltpu.VMEM((2, R, HD), BF16),
            pltpu.VMEM((8, T), F32),
            pltpu.VMEM((NH, 8, 128), F32),
            pltpu.VMEM((G, 8, 128), F32),
            pltpu.VMEM((NB, 8, 128), F32),
            dma((G,)), dma((G,)), dma((G,)), dma((G,)), dma((G,)), dma((G,)),
            dma((NB,)), dma((NB,)),
            dma((DS,)), dma((DS,)),
            dma((G,)), dma((G,)), dma((G,)), dma((G,)), dma((G,)), dma((G,)),
            dma((NH,)), dma((NH,)), dma((G,)), dma((G,)), dma((NB,)), dma((NB,)),
            dma((4,)),
        ],
        compiler_params=pltpu.CompilerParams(
            collective_id=0, has_side_effects=True, vmem_limit_bytes=56 * 1024 * 1024),
    )(window, queries, keys, values)
    return (loss[0, 0], dq.astype(F32), dk.astype(F32), dv.astype(F32))


def solution(mesh):
    return jax.shard_map(
        body,
        mesh=mesh,
        in_specs=(P("ctx", "head"), P("ctx", "head"), P("ctx", "head"), P("head")),
        out_specs=(P(), P("ctx", "head"), P("ctx", "head"), P("ctx", "head")),
        check_vma=False,
    )
```

```python
import functools
import math

import jax
import jax.numpy as jnp
from jax import lax
from jax.experimental import pallas as pl
from jax.experimental.pallas import tpu as pltpu
from jax.sharding import PartitionSpec as P

QH = 64
KVH = 8
HD = 128
WIN_MAX = 1024
WIN_MIN = 512
GS = QH // KVH
FWD_HEADS = 4
BWD_HEADS = 4

MESH = pl.DeviceIdType.MESH
NEG = -1e30
FLOOR = -1e20
F32 = jnp.float32
BF16 = jnp.bfloat16


def dot_nt(a, b):
    return lax.dot_general(a, b, (((1,), (1,)), ((), ())), preferred_element_type=F32)


def dot_nn(a, b):
    return jnp.dot(a, b, preferred_element_type=F32)


def kernel(
    G, NB, NH, SH, T, D,
    w_ref, q_ref, k_ref, v_ref,
    dq_out, dk_out, dv_out, loss_out,
    qs, kvs, kts, vts, o_near, o_far, stats, dos, dqs, dkv_acc, dkv_send, dkv_recv, dkv_fin, loss_acc, l_head, l_group, l_line,
    q_send, q_recv, k_send, k_recv, v_send, v_recv, kv_send, kv_recv,
    g_send, g_recv, dq_send, dq_recv, f_send, f_recv, e_send, e_recv, lh_send, lh_recv, lg_send, lg_recv, ll_send, ll_recv, loc,
):
    R = G * SH
    NT = R // T
    QW = GS * HD
    me = lax.axis_index("ctx")
    hd = lax.axis_index("head")
    z = me // G
    p = lax.rem(me, G)
    c = math.log2(math.e) / math.sqrt(HD)
    inv_root = 1.0 / math.sqrt(HD)

    def dev(zz, pp):
        return {"ctx": zz * G + pp}

    barrier = pltpu.get_barrier_semaphore()
    for o in range(1, G):
        pl.semaphore_signal(barrier, inc=1, device_id=dev(z, lax.rem(p + o, G)), device_id_type=MESH)

    def greet(o, carry):
        pl.semaphore_signal(barrier, inc=1, device_id=dev(lax.rem(z + o, NB), p), device_id_type=MESH)
        return carry

    lax.fori_loop(1, NB, greet, 0)
    for o in range(1, NH):
        pl.semaphore_signal(barrier, inc=1, device_id={"head": lax.rem(hd + o, NH)}, device_id_type=MESH)
    pl.semaphore_wait(barrier, G - 1 + NB - 1 + NH - 1)

    def my_rows(pp):
        return pl.ds(pl.multiple_of(pp * SH, SH), SH)

    def wide(pp):
        return pl.ds(pl.multiple_of(pp * QW, QW), QW)

    def narrow(pp):
        return pl.ds(pl.multiple_of(pp * HD, HD), HD)

    def kv_copy(src, part, o, send, recv):
        to = lax.rem(p + o, G)
        return pltpu.make_async_remote_copy(
            src_ref=src.at[:, narrow(to)],
            dst_ref=kvs.at[z, part, my_rows(p), :],
            send_sem=send.at[to], recv_sem=recv.at[p],
            device_id=dev(z, to), device_id_type=MESH)

    def q_copy(o):
        to = lax.rem(p + o, G)
        return pltpu.make_async_remote_copy(
            src_ref=q_ref.at[:, wide(to)],
            dst_ref=qs.at[my_rows(p), :],
            send_sem=q_send.at[to], recv_sem=q_recv.at[p],
            device_id=dev(z, to), device_id_type=MESH)

    def recv_kv(frm, part, recv):
        return pltpu.make_async_remote_copy(
            src_ref=kvs.at[z, part, my_rows(frm), :], dst_ref=kvs.at[z, part, my_rows(frm), :],
            send_sem=k_send.at[frm], recv_sem=recv.at[frm],
            device_id=dev(z, frm), device_id_type=MESH)

    for o in range(1, G):
        kv_copy(k_ref, 0, o, k_send, k_recv).start()
        kv_copy(v_ref, 1, o, v_send, v_recv).start()
    for o in range(1, G):
        q_copy(o).start()
    local = [
        pltpu.make_async_copy(k_ref.at[:, narrow(p)], kvs.at[z, 0, my_rows(p), :], loc.at[0]),
        pltpu.make_async_copy(v_ref.at[:, narrow(p)], kvs.at[z, 1, my_rows(p), :], loc.at[1]),
        pltpu.make_async_copy(q_ref.at[:, wide(p)], qs.at[my_rows(p), :], loc.at[2]),
    ]
    for one in local:
        one.start()

    stats[...] = jnp.zeros_like(stats)
    loss_acc[...] = jnp.zeros_like(loss_acc)

    def clear(h, carry):
        o_far[h] = jnp.zeros(o_far.shape[1:], F32)
        stats[h, pl.ds(2, 1), :] = jnp.full((1, R), FLOOR, F32)
        return carry

    lax.fori_loop(0, GS, clear, 0)

    for one in local:
        one.wait()
    for o in range(1, G):
        frm = lax.rem(p + o, G)
        recv_kv(frm, 0, k_recv).wait_recv()
        recv_kv(frm, 1, v_recv).wait_recv()

    def block_copy(src_block, to_z):
        return pltpu.make_async_remote_copy(
            src_ref=kvs.at[src_block], dst_ref=kvs.at[src_block],
            send_sem=kv_send.at[to_z], recv_sem=kv_recv.at[src_block],
            device_id=dev(to_z, p), device_id_type=MESH)

    def send_up(to_z, carry):
        block_copy(z, to_z).start()
        return carry

    lax.fori_loop(z + 1, NB, send_up, 0)
    for o in range(1, G):
        frm = lax.rem(p + o, G)
        pltpu.make_async_remote_copy(
            src_ref=qs.at[my_rows(frm), :], dst_ref=qs.at[my_rows(frm), :],
            send_sem=q_send.at[frm], recv_sem=q_recv.at[frm],
            device_id=dev(z, frm), device_id_type=MESH).wait_recv()

    window = w_ref[p]
    ramp = lax.broadcasted_iota(jnp.int32, (T, T), 1) - lax.broadcasted_iota(jnp.int32, (T, T), 0)

    def tiles_of(d, rt):
        found = []
        for kt in range(NT):
            delta = d * R + (rt - kt) * T
            if delta < 0:
                continue
            near = delta - (T - 1) < WIN_MAX
            far = delta + (T - 1) >= WIN_MIN
            found.append((kt, delta, near, far))
        return found

    def turn(ref_out, block, part):
        ref_out[...] = kvs[block, part].astype(F32).T.astype(BF16)

    def forward(h, d, rt, block, far_only=False):
        rows = slice(rt * T, (rt + 1) * T)
        q = qs[rows, narrow(h)]
        work = []
        for kt, delta, near, far in ([(kt, None, False, True) for kt in range(NT)] if far_only else tiles_of(d, rt)):
            keys = kvs[block, 0, kt * T:(kt + 1) * T, :]
            work.append((kt, delta, near, far, dot_nt(keys, q) * c))
        yield
        has_near = any(t[2] for t in work)
        has_far = any(t[3] for t in work)
        if has_near:
            m_s = None if d == 0 else stats[h, 0:1, rows]
            new_s = m_s
        if has_far:
            m_f = stats[h, 2:3, rows]
            new_f = m_f
        masks = []
        for kt, delta, near, far, s in work:
            mask = None
            if near and far:
                mask = ramp < window - delta
                s_near = jnp.where(mask, s, NEG)
                s_far = jnp.where(mask, NEG, s)
            elif near and delta == 0:
                s_near = jnp.where(ramp >= 0, s, NEG)
                mask = s_near
            else:
                s_near = s_far = s
            masks.append(mask)
            if near:
                top = jnp.max(s_near, axis=0, keepdims=True)
                new_s = top if new_s is None else jnp.maximum(new_s, top)
            if far:
                new_f = jnp.maximum(new_f, jnp.max(s_far, axis=0, keepdims=True))
        yield
        near_sum, far_sum, near_o, far_o = 0.0, 0.0, 0.0, 0.0
        for (kt, delta, near, far, s), mask in zip(work, masks):
            vt = vts[:, kt * T:(kt + 1) * T]
            if near and far:
                e = jnp.exp2(s - jnp.where(mask, new_s, new_f))
                p_near = jnp.where(mask, e, 0.0)
                p_far = jnp.where(mask, 0.0, e)
            elif near:
                p_near = jnp.exp2((mask if delta == 0 else s) - new_s)
            else:
                p_far = jnp.exp2(s - new_f)
            if near:
                near_sum = near_sum + jnp.sum(p_near, axis=0, keepdims=True)
                near_o = near_o + dot_nn(vt, p_near.astype(BF16))
            if far:
                far_sum = far_sum + jnp.sum(p_far, axis=0, keepdims=True)
                far_o = far_o + dot_nn(vt, p_far.astype(BF16))
        yield
        if has_near:
            if d == 0:
                stats[h, 1:2, rows] = near_sum
                o_near[h, :, rows] = near_o
            else:
                factor = jnp.exp2(m_s - new_s)
                stats[h, 1:2, rows] = stats[h, 1:2, rows] * factor + near_sum
                o_near[h, :, rows] = o_near[h, :, rows] * factor + near_o
            stats[h, 0:1, rows] = new_s
        if has_far:
            factor = jnp.exp2(m_f - new_f)
            stats[h, 3:4, rows] = stats[h, 3:4, rows] * factor + far_sum
            o_far[h, :, rows] = o_far[h, :, rows] * factor + far_o
            stats[h, 2:3, rows] = new_f

    def heads(fn, count=1, finish=None):
        def step(i, carry):
            running = [fn(i * count + j) for j in range(count)]
            if running[0] is not None:
                totals = []
                while running:
                    alive = []
                    for one in running:
                        try:
                            next(one)
                            alive.append(one)
                        except StopIteration as end:
                            if end.value is not None:
                                totals.append(end.value)
                    running = alive
                if finish is not None:
                    finish(totals)
            return carry
        lax.fori_loop(0, GS // count, step, 0)

    def arrive(block):
        block_copy(block, z).wait_recv()

    for d in range(0, min(D, NB - 1) + 1):
        @pl.when(z >= d)
        def _():
            block = z - d
            if d > 0:
                arrive(block)
            turn(vts, block, 1)
            for rt in range(NT):
                heads(lambda h: forward(h, d, rt, block), FWD_HEADS)

    if NB - 1 > D:
        def far_block(d, carry):
            block = z - d
            arrive(block)
            turn(vts, block, 1)
            for rt in range(NT):
                heads(lambda h: forward(h, None, rt, block, True), FWD_HEADS)
            return carry
        lax.fori_loop(D + 1, z + 1, far_block, 0)

    def middle(h, rt):
        rows = slice(rt * T, (rt + 1) * T)
        m_s, l_s = stats[h, 0:1, rows], stats[h, 1:2, rows]
        m_f, l_f = stats[h, 2:3, rows], stats[h, 3:4, rows]
        m_t = jnp.maximum(m_s, m_f)
        a_s, a_f = jnp.exp2(m_s - m_t), jnp.exp2(m_f - m_t)
        total = l_s * a_s + l_f * a_f
        near = o_near[h, :, rows]
        student = near / l_s
        teacher = (near * a_s + o_far[h, :, rows] * a_f) / total
        diff = student - teacher.astype(BF16).astype(F32)
        loss_acc[...] += jnp.sum((diff * diff).reshape(HD // 8, 8, T), axis=0)
        stats[h, 4:5, rows] = m_s + jnp.log2(l_s)
        stats[h, 5:6, rows] = jnp.sum(diff * student, axis=0, keepdims=True)
        dos[rows, narrow(h)] = diff.T.astype(BF16)
        o_near[h, :, rows] = jnp.zeros((HD, T), F32)

    for rt in range(NT):
        heads(lambda h: middle(h, rt))
    head_loss = loss_acc[:, 0:128]
    for lane in range(128, T, 128):
        head_loss = head_loss + loss_acc[:, lane:lane + 128]
    l_head[hd] = head_loss

    def loss_copies(buf, count, mine, send, recv, where):
        def one(o, carry, act):
            to = lax.rem(mine + o, count)
            act(pltpu.make_async_remote_copy(
                src_ref=buf.at[mine], dst_ref=buf.at[mine],
                send_sem=send.at[to], recv_sem=recv.at[mine],
                device_id=where(to), device_id_type=MESH))
            return carry

        def got(o, carry):
            frm = lax.rem(mine + o, count)
            pltpu.make_async_remote_copy(
                src_ref=buf.at[frm], dst_ref=buf.at[frm],
                send_sem=send.at[frm], recv_sem=recv.at[frm],
                device_id=where(frm), device_id_type=MESH).wait_recv()
            return carry

        def start():
            lax.fori_loop(1, count, functools.partial(one, act=lambda x: x.start()), 0)

        def total():
            lax.fori_loop(1, count, got, 0)
            return lax.fori_loop(1, count, lambda i, t: t + buf[i], buf[0])

        def drain():
            lax.fori_loop(1, count, functools.partial(one, act=lambda x: x.wait_send()), 0)

        return start, total, drain

    loss_head = loss_copies(l_head, NH, hd, lh_send, lh_recv, lambda to: {"head": to})
    loss_group = loss_copies(l_group, G, p, lg_send, lg_recv, lambda to: dev(z, to))
    loss_line = loss_copies(l_line, NB, z, ll_send, ll_recv, lambda to: dev(to, p))
    loss_head[0]()

    def backward(h, d, rt, block):
        rows = slice(rt * T, (rt + 1) * T)
        q = qs[rows, narrow(h)]
        do = dos[rows, narrow(h)]
        lse = stats[h, 4:5, rows]
        rd = stats[h, 5:6, rows]
        dq = o_near[h, :, rows]
        work = []
        for kt, delta, near, far in tiles_of(d, rt):
            if near:
                part = slice(kt * T, (kt + 1) * T)
                work.append((part, delta, far, dot_nt(kvs[block, 0, part, :], q) * c,
                             dot_nt(kvs[block, 1, part, :], do)))
        yield
        terms = []
        for part, delta, far, s, dp in work:
            if far:
                s = jnp.where(ramp < window - delta, s, NEG)
            elif delta == 0:
                s = jnp.where(ramp >= 0, s, NEG)
            w = jnp.exp2(s - lse)
            ds = (w * (dp - rd)).astype(BF16)
            dv = dot_nn(w.astype(BF16), do)
            dk = dot_nn(ds, q)
            dq = dq + dot_nn(kts[:, part], ds)
            terms.append((part, dk, dv))
        yield
        if d == 0:
            dqs[rows, narrow(h)] = (dq * inv_root).T.astype(BF16)
        else:
            o_near[h, :, rows] = dq
        return terms

    def add_terms(per_head):
        for same in zip(*per_head):
            part = same[0][0]
            dkv_acc[0, part, :] += sum(t[1] for t in same)
            dkv_acc[1, part, :] += sum(t[2] for t in same)

    def term_copy(d, to_z):
        return pltpu.make_async_remote_copy(
            src_ref=dkv_send.at[d - 1], dst_ref=dkv_recv.at[d - 1],
            send_sem=g_send.at[d - 1], recv_sem=g_recv.at[d - 1],
            device_id=dev(to_z, p), device_id_type=MESH)

    def dq_copy(to):
        return pltpu.make_async_remote_copy(
            src_ref=dqs.at[my_rows(to), :], dst_ref=dq_out.at[:, wide(p)],
            send_sem=dq_send.at[to], recv_sem=dq_recv.at[p],
            device_id=dev(z, to), device_id_type=MESH)

    def dq_local(to):
        return pltpu.make_async_copy(dqs.at[my_rows(to), :], dq_out.at[:, wide(p)], loc.at[2])

    def fin_copy(to, part):
        out, send, recv = ((dk_out, f_send, f_recv), (dv_out, e_send, e_recv))[part]
        return pltpu.make_async_remote_copy(
            src_ref=dkv_fin.at[part, my_rows(to), :], dst_ref=out.at[:, narrow(p)],
            send_sem=send.at[to], recv_sem=recv.at[p],
            device_id=dev(z, to), device_id_type=MESH)

    def fin_local(to, part):
        out = (dk_out, dv_out)[part]
        return pltpu.make_async_copy(
            dkv_fin.at[part, my_rows(to), :], out.at[:, narrow(p)], loc.at[part])

    for d in range(min(D, NB - 1), 0, -1):
        @pl.when(z >= d)
        def _():
            block = z - d
            dkv_acc[...] = jnp.zeros_like(dkv_acc)
            turn(kts, block, 0)
            for rt in range(NT):
                if any(t[2] for t in tiles_of(d, rt)):
                    heads(lambda h: backward(h, d, rt, block), BWD_HEADS, add_terms)
            dkv_send[d - 1, 0] = (dkv_acc[0] * inv_root).astype(BF16)
            dkv_send[d - 1, 1] = dkv_acc[1].astype(BF16)
            term_copy(d, z - d).start()

    l_group[p] = loss_head[1]()
    loss_group[0]()
    dkv_acc[...] = jnp.zeros_like(dkv_acc)
    turn(kts, z, 0)
    for rt in range(NT):
        heads(lambda h: backward(h, 0, rt, z), BWD_HEADS, add_terms)
        if rt == 0:
            l_line[z] = loss_group[1]()
            loss_line[0]()
        for to in range(rt * T // SH, (rt + 1) * T // SH):
            @pl.when(p != to)
            def _():
                dq_copy(to).start()

            @pl.when(p == to)
            def _():
                dq_local(to).start()

    dkv_acc[0] = dkv_acc[0] * inv_root
    for d in range(1, min(D, NB - 1) + 1):
        @pl.when(z + d < NB)
        def _():
            term_copy(d, z).wait_recv()
            dkv_acc[...] += dkv_recv[d - 1].astype(F32)
    dkv_fin[...] = dkv_acc[...].astype(BF16)
    for to in range(G):
        @pl.when(p != to)
        def _():
            fin_copy(to, 0).start()
            fin_copy(to, 1).start()

        @pl.when(p == to)
        def _():
            fin_local(to, 0).start()
            fin_local(to, 1).start()

    def drain_up(to_z, carry):
        block_copy(z, to_z).wait_send()
        return carry

    for o in range(1, G):
        kv_copy(k_ref, 0, o, k_send, k_recv).wait_send()
        kv_copy(v_ref, 1, o, v_send, v_recv).wait_send()
        q_copy(o).wait_send()
    lax.fori_loop(z + 1, NB, drain_up, 0)
    for d in range(1, min(D, NB - 1) + 1):
        @pl.when(z >= d)
        def _():
            term_copy(d, z - d).wait_send()
    dq_local(p).wait()
    fin_local(p, 0).wait()
    fin_local(p, 1).wait()
    loss_out[0, 0] = jnp.sum(loss_line[1]()) / (NB * R * QH * HD)
    for part in (loss_head, loss_group, loss_line):
        part[2]()
    for o in range(1, G):
        other = lax.rem(p + o, G)
        dq_copy(other).wait_send()
        for part in range(2):
            fin_copy(other, part).wait_send()
            out, send, recv = ((dk_out, f_send, f_recv), (dv_out, e_send, e_recv))[part]
            landed = out.at[:, narrow(other)]
            pltpu.make_async_remote_copy(
                src_ref=landed, dst_ref=landed, send_sem=send.at[other], recv_sem=recv.at[other],
                device_id=dev(z, other), device_id_type=MESH).wait_recv()
        landed = dq_out.at[:, wide(other)]
        pltpu.make_async_remote_copy(
            src_ref=landed, dst_ref=landed, send_sem=dq_send.at[other], recv_sem=dq_recv.at[other],
            device_id=dev(z, other), device_id_type=MESH).wait_recv()


def body(queries, keys, values, window):
    sh, key_width = keys.shape
    G = key_width // HD
    n_ctx = lax.axis_size("ctx")
    NB = n_ctx // G
    R = G * sh
    T = math.gcd(R, 256)
    D = (WIN_MAX - 1 + R - 1) // R
    DS = max(1, min(D, NB - 1))
    dma = pltpu.SemaphoreType.DMA
    any_spec = pl.BlockSpec(memory_space=pl.ANY)
    NH = lax.axis_size("head")
    dq, dk, dv, loss = pl.pallas_call(
        functools.partial(kernel, G, NB, NH, sh, T, D),
        out_shape=(
            jax.ShapeDtypeStruct((sh, G * GS * HD), BF16),
            jax.ShapeDtypeStruct((sh, G * HD), BF16),
            jax.ShapeDtypeStruct((sh, G * HD), BF16),
            jax.ShapeDtypeStruct((1, 1), F32),
        ),
        in_specs=[pl.BlockSpec(memory_space=pltpu.SMEM), any_spec, any_spec, any_spec],
        out_specs=(any_spec, any_spec, any_spec, pl.BlockSpec(memory_space=pltpu.SMEM)),
        scratch_shapes=[
            pltpu.VMEM((R, GS * HD), BF16),
            pltpu.VMEM((NB, 2, R, HD), BF16),
            pltpu.VMEM((HD, R), BF16),
            pltpu.VMEM((HD, R), BF16),
            pltpu.VMEM((GS, HD, R), F32),
            pltpu.VMEM((GS, HD, R), F32),
            pltpu.VMEM((GS, 8, R), F32),
            pltpu.VMEM((R, GS * HD), BF16),
            pltpu.VMEM((R, GS * HD), BF16),
            pltpu.VMEM((2, R, HD), F32),
            pltpu.VMEM((DS, 2, R, HD), BF16),
            pltpu.VMEM((DS, 2, R, HD), BF16),
            pltpu.VMEM((2, R, HD), BF16),
            pltpu.VMEM((8, T), F32),
            pltpu.VMEM((NH, 8, 128), F32),
            pltpu.VMEM((G, 8, 128), F32),
            pltpu.VMEM((NB, 8, 128), F32),
            dma((G,)), dma((G,)), dma((G,)), dma((G,)), dma((G,)), dma((G,)),
            dma((NB,)), dma((NB,)),
            dma((DS,)), dma((DS,)),
            dma((G,)), dma((G,)), dma((G,)), dma((G,)), dma((G,)), dma((G,)),
            dma((NH,)), dma((NH,)), dma((G,)), dma((G,)), dma((NB,)), dma((NB,)),
            dma((4,)),
        ],
        compiler_params=pltpu.CompilerParams(
            collective_id=0, has_side_effects=True, vmem_limit_bytes=56 * 1024 * 1024),
    )(window, queries, keys, values)
    return (loss[0, 0], dq.astype(F32), dk.astype(F32), dv.astype(F32))


def solution(mesh):
    return jax.shard_map(
        body,
        mesh=mesh,
        in_specs=(P("ctx", "head"), P("ctx", "head"), P("ctx", "head"), P("head")),
        out_specs=(P(), P("ctx", "head"), P("ctx", "head"), P("ctx", "head")),
        check_vma=False,
    )
```

```python
import functools
import math

import jax
import jax.numpy as jnp
from jax import lax
from jax.experimental import pallas as pl
from jax.experimental.pallas import tpu as pltpu
from jax.sharding import PartitionSpec as P

QH = 64
KVH = 8
HD = 128
WIN_MAX = 1024
WIN_MIN = 512
GS = QH // KVH
FWD_HEADS = 4
BWD_HEADS = 4
PARTS = 2

MESH = pl.DeviceIdType.MESH
NEG = -1e30
FLOOR = -1e20
F32 = jnp.float32
BF16 = jnp.bfloat16


def dot_nt(a, b):
    return lax.dot_general(a, b, (((1,), (1,)), ((), ())), preferred_element_type=F32)


def dot_nn(a, b):
    return jnp.dot(a, b, preferred_element_type=F32)


def kernel(
    G, NB, NH, SH, T, D,
    w_ref, q_ref, k_ref, v_ref,
    dq_out, dk_out, dv_out, loss_out,
    qs, kvs, kts, vts, o_near, o_far, stats, dos, dqs, dkv_acc, dkv_send, dkv_recv, dkv_fin, loss_acc, l_head, l_group, l_line,
    q_send, q_recv, k_send, k_recv, v_send, v_recv, kv_send, kv_recv,
    g_send, g_recv, dq_send, dq_recv, f_send, f_recv, e_send, e_recv, lh_send, lh_recv, lg_send, lg_recv, ll_send, ll_recv, loc,
):
    R = G * SH
    NT = R // T
    QW = GS * HD
    me = lax.axis_index("ctx")
    hd = lax.axis_index("head")
    z = me // G
    p = lax.rem(me, G)
    c = math.log2(math.e) / math.sqrt(HD)
    inv_root = 1.0 / math.sqrt(HD)

    def dev(zz, pp):
        return {"ctx": zz * G + pp}

    barrier = pltpu.get_barrier_semaphore()
    for o in range(1, G):
        pl.semaphore_signal(barrier, inc=1, device_id=dev(z, lax.rem(p + o, G)), device_id_type=MESH)

    def greet(o, carry):
        pl.semaphore_signal(barrier, inc=1, device_id=dev(lax.rem(z + o, NB), p), device_id_type=MESH)
        return carry

    lax.fori_loop(1, NB, greet, 0)
    for o in range(1, NH):
        pl.semaphore_signal(barrier, inc=1, device_id={"head": lax.rem(hd + o, NH)}, device_id_type=MESH)
    pl.semaphore_wait(barrier, G - 1 + NB - 1 + NH - 1)

    def my_rows(pp):
        return pl.ds(pl.multiple_of(pp * SH, SH), SH)

    def wide(pp):
        return pl.ds(pl.multiple_of(pp * QW, QW), QW)

    def narrow(pp):
        return pl.ds(pl.multiple_of(pp * HD, HD), HD)

    def kv_copy(src, part, o, send, recv):
        to = lax.rem(p + o, G)
        return pltpu.make_async_remote_copy(
            src_ref=src.at[:, narrow(to)],
            dst_ref=kvs.at[z, part, my_rows(p), :],
            send_sem=send.at[to], recv_sem=recv.at[p],
            device_id=dev(z, to), device_id_type=MESH)

    PW = QW // PARTS
    PH = GS // PARTS

    def part_of(pp, part):
        return pl.ds(pl.multiple_of(pp * QW + part * PW, PW), PW)

    def q_copy(o, part):
        to = lax.rem(p + o, G)
        return pltpu.make_async_remote_copy(
            src_ref=q_ref.at[:, part_of(to, part)],
            dst_ref=qs.at[my_rows(p), part_of(0, part)],
            send_sem=q_send.at[part, to], recv_sem=q_recv.at[part, p],
            device_id=dev(z, to), device_id_type=MESH)

    def recv_kv(frm, part, recv):
        return pltpu.make_async_remote_copy(
            src_ref=kvs.at[z, part, my_rows(frm), :], dst_ref=kvs.at[z, part, my_rows(frm), :],
            send_sem=k_send.at[frm], recv_sem=recv.at[frm],
            device_id=dev(z, frm), device_id_type=MESH)

    for o in range(1, G):
        kv_copy(k_ref, 0, o, k_send, k_recv).start()
        kv_copy(v_ref, 1, o, v_send, v_recv).start()
    for part in range(PARTS):
        for o in range(1, G):
            q_copy(o, part).start()
    local = [
        pltpu.make_async_copy(k_ref.at[:, narrow(p)], kvs.at[z, 0, my_rows(p), :], loc.at[0]),
        pltpu.make_async_copy(v_ref.at[:, narrow(p)], kvs.at[z, 1, my_rows(p), :], loc.at[1]),
        pltpu.make_async_copy(q_ref.at[:, wide(p)], qs.at[my_rows(p), :], loc.at[2]),
    ]
    for one in local:
        one.start()

    stats[...] = jnp.zeros_like(stats)
    loss_acc[...] = jnp.zeros_like(loss_acc)

    def clear(h, carry):
        o_far[h] = jnp.zeros(o_far.shape[1:], F32)
        stats[h, pl.ds(2, 1), :] = jnp.full((1, R), FLOOR, F32)
        return carry

    lax.fori_loop(0, GS, clear, 0)

    for one in local:
        one.wait()
    for o in range(1, G):
        frm = lax.rem(p + o, G)
        recv_kv(frm, 0, k_recv).wait_recv()
        recv_kv(frm, 1, v_recv).wait_recv()

    def block_copy(src_block, to_z):
        return pltpu.make_async_remote_copy(
            src_ref=kvs.at[src_block], dst_ref=kvs.at[src_block],
            send_sem=kv_send.at[to_z], recv_sem=kv_recv.at[src_block],
            device_id=dev(to_z, p), device_id_type=MESH)

    def send_up(to_z, carry):
        block_copy(z, to_z).start()
        return carry

    lax.fori_loop(z + 1, NB, send_up, 0)

    def q_arrive(part):
        for o in range(1, G):
            frm = lax.rem(p + o, G)
            landed = qs.at[my_rows(frm), part_of(0, part)]
            pltpu.make_async_remote_copy(
                src_ref=landed, dst_ref=landed,
                send_sem=q_send.at[part, frm], recv_sem=q_recv.at[part, frm],
                device_id=dev(z, frm), device_id_type=MESH).wait_recv()

    window = w_ref[p]
    ramp = lax.broadcasted_iota(jnp.int32, (T, T), 1) - lax.broadcasted_iota(jnp.int32, (T, T), 0)

    def tiles_of(d, rt):
        found = []
        for kt in range(NT):
            delta = d * R + (rt - kt) * T
            if delta < 0:
                continue
            near = delta - (T - 1) < WIN_MAX
            far = delta + (T - 1) >= WIN_MIN
            found.append((kt, delta, near, far))
        return found

    def turn(ref_out, block, part):
        ref_out[...] = kvs[block, part].astype(F32).T.astype(BF16)

    def forward(h, d, rt, block, far_only=False):
        rows = slice(rt * T, (rt + 1) * T)
        q = qs[rows, narrow(h)]
        work = []
        for kt, delta, near, far in ([(kt, None, False, True) for kt in range(NT)] if far_only else tiles_of(d, rt)):
            keys = kvs[block, 0, kt * T:(kt + 1) * T, :]
            work.append((kt, delta, near, far, dot_nt(keys, q) * c))
        yield
        has_near = any(t[2] for t in work)
        has_far = any(t[3] for t in work)
        if has_near:
            m_s = None if d == 0 else stats[h, 0:1, rows]
            new_s = m_s
        if has_far:
            m_f = stats[h, 2:3, rows]
            new_f = m_f
        masks = []
        for kt, delta, near, far, s in work:
            mask = None
            if near and far:
                mask = ramp < window - delta
                s_near = jnp.where(mask, s, NEG)
                s_far = jnp.where(mask, NEG, s)
            elif near and delta == 0:
                s_near = jnp.where(ramp >= 0, s, NEG)
                mask = s_near
            else:
                s_near = s_far = s
            masks.append(mask)
            if near:
                top = jnp.max(s_near, axis=0, keepdims=True)
                new_s = top if new_s is None else jnp.maximum(new_s, top)
            if far:
                new_f = jnp.maximum(new_f, jnp.max(s_far, axis=0, keepdims=True))
        yield
        near_sum, far_sum, near_o, far_o = 0.0, 0.0, 0.0, 0.0
        for (kt, delta, near, far, s), mask in zip(work, masks):
            vt = vts[:, kt * T:(kt + 1) * T]
            if near and far:
                e = jnp.exp2(s - jnp.where(mask, new_s, new_f))
                p_near = jnp.where(mask, e, 0.0)
                p_far = jnp.where(mask, 0.0, e)
            elif near:
                p_near = jnp.exp2((mask if delta == 0 else s) - new_s)
            else:
                p_far = jnp.exp2(s - new_f)
            if near:
                near_sum = near_sum + jnp.sum(p_near, axis=0, keepdims=True)
                near_o = near_o + dot_nn(vt, p_near.astype(BF16))
            if far:
                far_sum = far_sum + jnp.sum(p_far, axis=0, keepdims=True)
                far_o = far_o + dot_nn(vt, p_far.astype(BF16))
        yield
        if has_near:
            if d == 0:
                stats[h, 1:2, rows] = near_sum
                o_near[h, :, rows] = near_o
            else:
                factor = jnp.exp2(m_s - new_s)
                stats[h, 1:2, rows] = stats[h, 1:2, rows] * factor + near_sum
                o_near[h, :, rows] = o_near[h, :, rows] * factor + near_o
            stats[h, 0:1, rows] = new_s
        if has_far:
            factor = jnp.exp2(m_f - new_f)
            stats[h, 3:4, rows] = stats[h, 3:4, rows] * factor + far_sum
            o_far[h, :, rows] = o_far[h, :, rows] * factor + far_o
            stats[h, 2:3, rows] = new_f

    def heads(fn, count=1, finish=None, low=0, high=GS):
        def step(i, carry):
            running = [fn(i * count + j) for j in range(count)]
            if running[0] is not None:
                totals = []
                while running:
                    alive = []
                    for one in running:
                        try:
                            next(one)
                            alive.append(one)
                        except StopIteration as end:
                            if end.value is not None:
                                totals.append(end.value)
                    running = alive
                if finish is not None:
                    finish(totals)
            return carry
        lax.fori_loop(low // count, high // count, step, 0)

    def arrive(block):
        block_copy(block, z).wait_recv()

    for d in range(0, min(D, NB - 1) + 1):
        @pl.when(z >= d)
        def _():
            block = z - d
            if d > 0:
                arrive(block)
                turn(vts, block, 1)
                for rt in range(NT):
                    heads(lambda h: forward(h, d, rt, block), FWD_HEADS)
            else:
                turn(vts, block, 1)
                turn(kts.at[0], block, 0)
                for part in range(PARTS):
                    q_arrive(part)
                    for rt in range(NT):
                        heads(lambda h: forward(h, d, rt, block), FWD_HEADS, None, part * PH, part * PH + PH)

    if NB - 1 > D:
        def far_block(d, carry):
            block = z - d
            arrive(block)
            turn(vts, block, 1)
            for rt in range(NT):
                heads(lambda h: forward(h, None, rt, block, True), FWD_HEADS)
            return carry
        lax.fori_loop(D + 1, z + 1, far_block, 0)

    def middle(h, rt):
        rows = slice(rt * T, (rt + 1) * T)
        m_s, l_s = stats[h, 0:1, rows], stats[h, 1:2, rows]
        m_f, l_f = stats[h, 2:3, rows], stats[h, 3:4, rows]
        m_t = jnp.maximum(m_s, m_f)
        a_s, a_f = jnp.exp2(m_s - m_t), jnp.exp2(m_f - m_t)
        total = l_s * a_s + l_f * a_f
        near = o_near[h, :, rows]
        student = near * (1.0 / l_s)
        teacher = near * (a_s / total) + o_far[h, :, rows] * (a_f / total)
        diff = student - teacher.astype(BF16).astype(F32)
        squares = jnp.sum((diff * diff).reshape(HD // 8, 8, T), axis=0)
        yield
        loss_acc[...] += squares
        stats[h, 4:5, rows] = m_s + jnp.log2(l_s)
        stats[h, 5:6, rows] = jnp.sum(diff * student, axis=0, keepdims=True)
        dos[rows, narrow(h)] = diff.T.astype(BF16)
        o_near[h, :, rows] = jnp.zeros((HD, T), F32)

    for rt in range(NT):
        heads(lambda h: middle(h, rt), FWD_HEADS)
    head_loss = loss_acc[:, 0:128]
    for lane in range(128, T, 128):
        head_loss = head_loss + loss_acc[:, lane:lane + 128]
    l_head[hd] = head_loss

    def loss_copies(buf, count, mine, send, recv, where):
        def one(o, carry, act):
            to = lax.rem(mine + o, count)
            act(pltpu.make_async_remote_copy(
                src_ref=buf.at[mine], dst_ref=buf.at[mine],
                send_sem=send.at[to], recv_sem=recv.at[mine],
                device_id=where(to), device_id_type=MESH))
            return carry

        def got(o, carry):
            frm = lax.rem(mine + o, count)
            pltpu.make_async_remote_copy(
                src_ref=buf.at[frm], dst_ref=buf.at[frm],
                send_sem=send.at[frm], recv_sem=recv.at[frm],
                device_id=where(frm), device_id_type=MESH).wait_recv()
            return carry

        def start():
            lax.fori_loop(1, count, functools.partial(one, act=lambda x: x.start()), 0)

        def total():
            lax.fori_loop(1, count, got, 0)
            return lax.fori_loop(1, count, lambda i, t: t + buf[i], buf[0])

        def drain():
            lax.fori_loop(1, count, functools.partial(one, act=lambda x: x.wait_send()), 0)

        return start, total, drain

    loss_head = loss_copies(l_head, NH, hd, lh_send, lh_recv, lambda to: {"head": to})
    loss_group = loss_copies(l_group, G, p, lg_send, lg_recv, lambda to: dev(z, to))
    loss_line = loss_copies(l_line, NB, z, ll_send, ll_recv, lambda to: dev(to, p))
    loss_head[0]()

    def backward(h, d, rt, block):
        rows = slice(rt * T, (rt + 1) * T)
        q = qs[rows, narrow(h)]
        do = dos[rows, narrow(h)]
        lse = stats[h, 4:5, rows]
        rd = stats[h, 5:6, rows]
        dq = o_near[h, :, rows]
        work = []
        for kt, delta, near, far in tiles_of(d, rt):
            if near:
                part = slice(kt * T, (kt + 1) * T)
                work.append((part, delta, far, dot_nt(kvs[block, 0, part, :], q) * c,
                             dot_nt(kvs[block, 1, part, :], do)))
        yield
        terms = []
        for part, delta, far, s, dp in work:
            if far:
                s = jnp.where(ramp < window - delta, s, NEG)
            elif delta == 0:
                s = jnp.where(ramp >= 0, s, NEG)
            w = jnp.exp2(s - lse)
            ds = (w * (dp - rd)).astype(BF16)
            dv = dot_nn(w.astype(BF16), do)
            dk = dot_nn(ds, q)
            dq = dq + dot_nn(kts[min(d, 1), :, part], ds)
            terms.append((dkv_acc.at[min(d, 1)], part, dk, dv))
        yield
        if d == 0:
            dqs[rows, narrow(h)] = (dq * inv_root).T.astype(BF16)
        else:
            o_near[h, :, rows] = dq
        return terms

    def add_terms(per_head):
        for same in zip(*per_head):
            acc, part = same[0][:2]
            acc[0, part, :] += sum(t[2] for t in same)
            acc[1, part, :] += sum(t[3] for t in same)

    def term_copy(d, to_z):
        return pltpu.make_async_remote_copy(
            src_ref=dkv_send.at[d - 1], dst_ref=dkv_recv.at[d - 1],
            send_sem=g_send.at[d - 1], recv_sem=g_recv.at[d - 1],
            device_id=dev(to_z, p), device_id_type=MESH)

    def dq_copy(to, part):
        return pltpu.make_async_remote_copy(
            src_ref=dqs.at[my_rows(to), part_of(0, part)], dst_ref=dq_out.at[:, part_of(p, part)],
            send_sem=dq_send.at[part, to], recv_sem=dq_recv.at[part, p],
            device_id=dev(z, to), device_id_type=MESH)

    def dq_local(to, part):
        return pltpu.make_async_copy(
            dqs.at[my_rows(to), part_of(0, part)], dq_out.at[:, part_of(p, part)], loc.at[2 + part])

    def fin_copy(to, part):
        out, send, recv = ((dk_out, f_send, f_recv), (dv_out, e_send, e_recv))[part]
        return pltpu.make_async_remote_copy(
            src_ref=dkv_fin.at[part, my_rows(to), :], dst_ref=out.at[:, narrow(p)],
            send_sem=send.at[to], recv_sem=recv.at[p],
            device_id=dev(z, to), device_id_type=MESH)

    def fin_local(to, part):
        out = (dk_out, dv_out)[part]
        return pltpu.make_async_copy(
            dkv_fin.at[part, my_rows(to), :], out.at[:, narrow(p)], loc.at[part])

    def back(d, part):
        for rt in range(NT):
            if any(t[2] for t in tiles_of(d, rt)):
                if part is None:
                    heads(lambda h: backward(h, d, rt, z - d), BWD_HEADS, add_terms)
                else:
                    heads(lambda h: backward(h, d, rt, z - d), BWD_HEADS, add_terms, part * PH, part * PH + PH)

    def send_term(d):
        dkv_send[d - 1, 0] = (dkv_acc[1, 0] * inv_root).astype(BF16)
        dkv_send[d - 1, 1] = dkv_acc[1, 1].astype(BF16)
        term_copy(d, z - d).start()

    top = min(D, NB - 1)
    dkv_acc[0] = jnp.zeros(dkv_acc.shape[1:], F32)
    for d in range(top, 0, -1):
        @pl.when(z >= d)
        def _():
            dkv_acc[1] = jnp.zeros(dkv_acc.shape[1:], F32)
            turn(kts.at[1], z - d, 0)
            if d > 1:
                back(d, None)
                send_term(d)

    l_group[p] = loss_head[1]()
    loss_group[0]()
    for part in range(PARTS):
        if top > 0:
            @pl.when(z >= 1)
            def _():
                back(1, part)
                if part == PARTS - 1:
                    send_term(1)
        back(0, part)
        if part == 0:
            l_line[z] = loss_group[1]()
            loss_line[0]()
        for o in range(1, G):
            dq_copy(lax.rem(p + o, G), part).start()
        dq_local(p, part).start()

    dkv_acc[0, 0] = dkv_acc[0, 0] * inv_root
    for d in range(top, 0, -1):
        @pl.when(z + d < NB)
        def _():
            term_copy(d, z).wait_recv()
            dkv_acc[0] += dkv_recv[d - 1].astype(F32)
    dkv_fin[...] = dkv_acc[0].astype(BF16)
    for to in range(G):
        @pl.when(p != to)
        def _():
            fin_copy(to, 0).start()
            fin_copy(to, 1).start()

        @pl.when(p == to)
        def _():
            fin_local(to, 0).start()
            fin_local(to, 1).start()

    def drain_up(to_z, carry):
        block_copy(z, to_z).wait_send()
        return carry

    for o in range(1, G):
        kv_copy(k_ref, 0, o, k_send, k_recv).wait_send()
        kv_copy(v_ref, 1, o, v_send, v_recv).wait_send()
        for part in range(PARTS):
            q_copy(o, part).wait_send()
    lax.fori_loop(z + 1, NB, drain_up, 0)
    for d in range(1, min(D, NB - 1) + 1):
        @pl.when(z >= d)
        def _():
            term_copy(d, z - d).wait_send()
    for part in range(PARTS):
        dq_local(p, part).wait()
    fin_local(p, 0).wait()
    fin_local(p, 1).wait()
    loss_out[0, 0] = jnp.sum(loss_line[1]()) / (NB * R * QH * HD)
    for part in (loss_head, loss_group, loss_line):
        part[2]()
    for o in range(1, G):
        other = lax.rem(p + o, G)
        for part in range(PARTS):
            dq_copy(other, part).wait_send()
            landed = dq_out.at[:, part_of(other, part)]
            pltpu.make_async_remote_copy(
                src_ref=landed, dst_ref=landed,
                send_sem=dq_send.at[part, other], recv_sem=dq_recv.at[part, other],
                device_id=dev(z, other), device_id_type=MESH).wait_recv()
        for part in range(2):
            fin_copy(other, part).wait_send()
            out, send, recv = ((dk_out, f_send, f_recv), (dv_out, e_send, e_recv))[part]
            landed = out.at[:, narrow(other)]
            pltpu.make_async_remote_copy(
                src_ref=landed, dst_ref=landed, send_sem=send.at[other], recv_sem=recv.at[other],
                device_id=dev(z, other), device_id_type=MESH).wait_recv()


def body(queries, keys, values, window):
    sh, key_width = keys.shape
    G = key_width // HD
    n_ctx = lax.axis_size("ctx")
    NB = n_ctx // G
    R = G * sh
    T = math.gcd(R, 256)
    D = (WIN_MAX - 1 + R - 1) // R
    DS = max(1, min(D, NB - 1))
    dma = pltpu.SemaphoreType.DMA
    any_spec = pl.BlockSpec(memory_space=pl.ANY)
    NH = lax.axis_size("head")
    dq, dk, dv, loss = pl.pallas_call(
        functools.partial(kernel, G, NB, NH, sh, T, D),
        out_shape=(
            jax.ShapeDtypeStruct((sh, G * GS * HD), BF16),
            jax.ShapeDtypeStruct((sh, G * HD), BF16),
            jax.ShapeDtypeStruct((sh, G * HD), BF16),
            jax.ShapeDtypeStruct((1, 1), F32),
        ),
        in_specs=[pl.BlockSpec(memory_space=pltpu.SMEM), any_spec, any_spec, any_spec],
        out_specs=(any_spec, any_spec, any_spec, pl.BlockSpec(memory_space=pltpu.SMEM)),
        scratch_shapes=[
            pltpu.VMEM((R, GS * HD), BF16),
            pltpu.VMEM((NB, 2, R, HD), BF16),
            pltpu.VMEM((2, HD, R), BF16),
            pltpu.VMEM((HD, R), BF16),
            pltpu.VMEM((GS, HD, R), F32),
            pltpu.VMEM((GS, HD, R), F32),
            pltpu.VMEM((GS, 8, R), F32),
            pltpu.VMEM((R, GS * HD), BF16),
            pltpu.VMEM((R, GS * HD), BF16),
            pltpu.VMEM((2, 2, R, HD), F32),
            pltpu.VMEM((DS, 2, R, HD), BF16),
            pltpu.VMEM((DS, 2, R, HD), BF16),
            pltpu.VMEM((2, R, HD), BF16),
            pltpu.VMEM((8, T), F32),
            pltpu.VMEM((NH, 8, 128), F32),
            pltpu.VMEM((G, 8, 128), F32),
            pltpu.VMEM((NB, 8, 128), F32),
            dma((PARTS, G)), dma((PARTS, G)), dma((G,)), dma((G,)), dma((G,)), dma((G,)),
            dma((NB,)), dma((NB,)),
            dma((DS,)), dma((DS,)),
            dma((PARTS, G)), dma((PARTS, G)), dma((G,)), dma((G,)), dma((G,)), dma((G,)),
            dma((NH,)), dma((NH,)), dma((G,)), dma((G,)), dma((NB,)), dma((NB,)),
            dma((2 + PARTS,)),
        ],
        compiler_params=pltpu.CompilerParams(
            collective_id=0, has_side_effects=True, vmem_limit_bytes=56 * 1024 * 1024),
    )(window, queries, keys, values)
    return (loss[0, 0], dq.astype(F32), dk.astype(F32), dv.astype(F32))


def solution(mesh):
    return jax.shard_map(
        body,
        mesh=mesh,
        in_specs=(P("ctx", "head"), P("ctx", "head"), P("ctx", "head"), P("head")),
        out_specs=(P(), P("ctx", "head"), P("ctx", "head"), P("ctx", "head")),
        check_vma=False,
    )
```
